32 devices in a mesh: blk: 2 (over x), grid: 16 (over z, y, core).
Axes of the slice: x: 2, y: 2, z: 4, core: 2. Of those that a mesh axis runs over, the one named last changes fastest.
Arguments:
- centers: bfloat16 [4096, 512], P(('blk', 'grid')), as said below
- weights: float32 [4096, 1000], P(('blk', 'grid')), may hold values from -6 to 6
- batch_index: int32 [512], replicated, may hold values from 0 to 4095, as said below
- labels: int32 [512], replicated, may hold values from 0 to 999
- sub_index: int32 [256], P(('blk', 'grid')), may hold values from 0 to 127
- eigvecs: bfloat16 [256, 160], P(('blk', 'grid')), may hold values from -0.375 to 0.375
- scales: float32 [160], replicated, may hold values from 1 to 16
Outputs:
- predictions: bfloat16 [512, 1000], replicated
- center_grad: bfloat16 [4096, 1000], P(('blk', 'grid'))
- sub_increment: float32 [256, 1000], P(('blk', 'grid'))
The draws below stay inside these ranges and needn't reach their ends.
Inputs may be any that keep to these rules, and one draw needn't show every extreme that they name: Each device's block of 128 centers is named by exactly 512 / 32 entries of batch_index. sub_index: entry i names center (i // 8) * 128 + sub_index[i]. centers: row scales of order one.
All inputs are finite; a program needn't handle non-finite values.
Results may differ from the reference program's by a relative error of at most 0.0011.
The reference program's roundings to bfloat16 on the way (of `batch`, `kbz`, `resid`, `subset`, `ksb` and `kzs`) count: a program that leaves them out, or rounds other values in their place, can miss the bound.
Values may be sent and summed in bfloat16 or wider, within the bound.
A program may use at most 64 MiB of HBM per device.

```python
import math
import jax
import jax.numpy as jnp
from jax import lax

D = 512
C = 1000
RANK = 160
B = 512
CENTER_DEV = 128
SUB_DEV = 8
GROUPS = 32
CENTERS = 4096
SUBSET = 256
N_BLK = 2
N_GRID = 16


def draw_centers(key, part):
    first = jax.random.fold_in(key, 11)
    second = jax.random.fold_in(key, 12)
    row_scale = jnp.exp(jax.random.uniform(first, (CENTERS, 1), jnp.float32, jnp.log(0.25), 0.0))
    values = jax.random.normal(second, (CENTERS, D), jnp.float32)
    return (row_scale * values).astype(jnp.bfloat16)


def draw_batch_index(key, part):
    first = jax.random.fold_in(key, 21)
    second = jax.random.fold_in(key, 22)
    share = B // GROUPS
    owners = jnp.repeat(jnp.arange(GROUPS, dtype=jnp.int32), share, total_repeat_length=B)
    owners = jax.random.permutation(first, owners)
    within = jax.random.randint(second, (B,), 0, CENTER_DEV, jnp.int32)
    return (owners * CENTER_DEV + within).astype(jnp.int32)


def with_ends(array, stream_key, least, largest):
    place = [jax.random.randint(jax.random.fold_in(stream_key, axis), (), 0, length) for axis, length in enumerate(array.shape)]
    main_axis = array.shape.index(max(array.shape))
    next_to = place[:main_axis] + [(place[main_axis] + 1) % array.shape[main_axis]] + place[main_axis + 1:]
    return array.at[tuple(place)].set(least).at[tuple(next_to)].set(largest)


def block_scale(own_key, dims, split, low, largest):
    gain = 1.0
    for dim, shards_of in split:
        steps = jax.random.uniform(jax.random.fold_in(jax.random.fold_in(own_key, 6), dim), (shards_of,), jnp.float32, low / len(split), largest / len(split))
        gain = gain * jnp.repeat(jnp.exp(steps), dims[dim] // shards_of).reshape((-1,) + (1,) * (len(dims) - 1 - dim))
    return gain


def noise(own_key, dims, scale, reach, cuts=(), held_as=jnp.bfloat16):
    level = block_scale(own_key, dims, cuts, -0.22, 0.18) if cuts else 1.0
    array = jax.random.normal(own_key, dims, jnp.float32) * scale * level
    return jnp.minimum(jnp.maximum(array, -reach), reach).astype(held_as)


def setup_inputs(seed: int = 0) -> dict:
    key_of = jax.random.split(jax.random.key(seed), 8)
    centers = draw_centers(jax.random.fold_in(key_of[7], 71), 0)
    weights = noise(key_of[1], (CENTERS, C), (D * (CENTER_DEV * N_BLK * N_GRID) ** -0.5 / 8), 6.0, ((0, 32),), jnp.float32)
    batch_index = draw_batch_index(jax.random.fold_in(key_of[7], 71), 0)
    labels = with_ends(jax.random.randint(key_of[3], (B,), 0, C), jax.random.fold_in(key_of[3], 1), 0, C - 1).astype(jnp.int32)
    sub_index = with_ends(jax.random.randint(key_of[4], (SUBSET,), 0, CENTER_DEV), jax.random.fold_in(key_of[4], 1), 0, CENTER_DEV - 1).astype(jnp.int32)
    eigvecs = noise(key_of[5], (SUBSET, RANK), SUBSET ** -0.5, 0.375, ((0, 32),))
    scales = jnp.clip(jnp.exp(jax.random.uniform(key_of[6], (RANK,), jnp.float32, math.log(1.0), math.log(16.0))), 1.0, 16.0)
    return {"centers": centers, "weights": weights, "batch_index": batch_index, "labels": labels, "sub_index": sub_index, "eigvecs": eigvecs, "scales": scales}


SOFTEN = 1.0
SPREAD = 4.0

def kernel(left, right):
    left_sq = lax.optimization_barrier(jnp.sum(jnp.square(left.astype(jnp.float32)), axis=1))
    right_sq = lax.optimization_barrier(jnp.sum(jnp.square(right.astype(jnp.float32)), axis=1))
    cross = lax.dot_general(left, right, (((1,), (1,)), ((), ())), preferred_element_type=jnp.float32)
    dist = jnp.sqrt(jnp.maximum(left_sq[:, None] + right_sq[None, :] - 2.0 * cross, 0.0) + SOFTEN)
    return jnp.exp(-dist / SPREAD)

def reference(centers, weights, batch_index, labels, sub_index, eigvecs, scales):
    groups = N_BLK * N_GRID
    batch = jnp.take(centers, batch_index, axis=0)
    blocks_z = centers.reshape(groups, CENTER_DEV, D)
    blocks_w = weights.reshape(groups, CENTER_DEV, C)

    def accumulate(carry, item):
        zrows, wrows = item
        kbz = kernel(batch, zrows).astype(jnp.bfloat16)
        return (carry + jnp.dot(kbz, wrows.astype(jnp.bfloat16), preferred_element_type=jnp.float32), None)
    total, unused = lax.scan(accumulate, jnp.zeros((B, C), jnp.float32), (blocks_z, blocks_w))
    predictions = total.astype(jnp.bfloat16)
    onehot = (labels[:, None] == jnp.arange(C, dtype=jnp.int32)[None, :]).astype(jnp.float32)
    resid = (total - onehot).astype(jnp.bfloat16)
    rows = (jnp.arange(SUBSET, dtype=jnp.int32) // SUB_DEV * CENTER_DEV + sub_index).astype(jnp.int32)
    subset = jnp.take(centers, rows, axis=0)
    ksb = kernel(subset, batch).astype(jnp.bfloat16)
    inner = jnp.dot(ksb, resid, preferred_element_type=jnp.float32)
    coeff = jnp.dot(eigvecs.astype(jnp.float32).T, inner, precision=lax.Precision.HIGHEST)
    scaled = scales[:, None] * coeff
    sub_increment = jnp.dot(eigvecs.astype(jnp.float32), scaled, precision=lax.Precision.HIGHEST)

    def gradient(zrows):
        kbz = kernel(batch, zrows).astype(jnp.bfloat16)
        first = lax.dot_general(kbz, resid, (((0,), (0,)), ((), ())), preferred_element_type=jnp.float32)
        kzs = kernel(zrows, subset).astype(jnp.bfloat16)
        kze = jnp.dot(kzs, eigvecs, preferred_element_type=jnp.float32)
        correction = jnp.dot(kze, scaled, precision=lax.Precision.HIGHEST)
        return (first - correction).astype(jnp.bfloat16)
    center_grad = lax.map(gradient, blocks_z).reshape(CENTERS, C)
    return (predictions, center_grad, sub_increment)
```

```python
import functools

import jax
import jax.numpy as jnp
from jax import lax
from jax.experimental import pallas as pl
from jax.experimental.pallas import tpu as pltpu
from jax.sharding import PartitionSpec as P

SOFTEN = 1.0
SPREAD = 4.0
CORES = 2
MESH = pl.DeviceIdType.MESH
F32 = jnp.float32
BF16 = jnp.bfloat16
HIGHEST = lax.Precision.HIGHEST


def kernel(left, right):
    left_sq = jnp.sum(jnp.square(left.astype(jnp.float32)), axis=1)
    right_sq = jnp.sum(jnp.square(right.astype(jnp.float32)), axis=1)
    cross = lax.dot_general(
        left, right, (((1,), (1,)), ((), ())), preferred_element_type=jnp.float32
    )
    dist = jnp.sqrt(jnp.maximum(left_sq[:, None] + right_sq[None, :] - 2.0 * cross, 0.0) + SOFTEN)
    return jnp.exp(-dist / SPREAD)


def one_hot(label_rows, classes):
    return (label_rows[:, None] == jnp.arange(classes, dtype=jnp.int32)[None, :]).astype(
        jnp.float32
    )


def local(centers, weights, batch_index, labels, sub_index, eigvecs, scales):
    myself = lax.axis_index(("blk", "grid"))
    held = centers.shape[0]
    classes = weights.shape[1]
    owner = batch_index // held
    within = batch_index % held
    picked = jnp.take(centers, within, axis=0).astype(jnp.float32)
    picked = jnp.where((owner == myself)[:, None], picked, 0.0)
    batch = lax.psum(picked, ("blk", "grid")).astype(jnp.bfloat16)
    kbz = kernel(batch, centers).astype(jnp.bfloat16)
    partial_out = jnp.dot(kbz, weights.astype(jnp.bfloat16), preferred_element_type=jnp.float32)
    total = lax.psum(partial_out, ("blk", "grid"))
    predictions = total.astype(jnp.bfloat16)
    resid = (total - one_hot(labels, classes)).astype(jnp.bfloat16)
    subset_here = jnp.take(centers, sub_index, axis=0)
    sub_rows = lax.all_gather(subset_here, ("blk", "grid"), axis=0, tiled=True)
    vec_rows = lax.all_gather(eigvecs, ("blk", "grid"), axis=0, tiled=True)
    kzs = kernel(centers, sub_rows).astype(jnp.bfloat16)
    ksb_piece = kernel(sub_rows, batch).astype(jnp.bfloat16)
    kze_next = jnp.dot(kzs, vec_rows, preferred_element_type=jnp.float32)
    proj_next = lax.dot_general(
        vec_rows, ksb_piece, (((0,), (0,)), ((), ())), preferred_element_type=jnp.float32
    )
    coeff = jnp.dot(proj_next, resid.astype(jnp.float32), precision=lax.Precision.HIGHEST)
    scaled = scales[:, None] * coeff
    sub_increment = jnp.dot(eigvecs.astype(jnp.float32), scaled, precision=lax.Precision.HIGHEST)
    correction = jnp.dot(kze_next, scaled, precision=lax.Precision.HIGHEST)
    first = lax.dot_general(
        kbz, resid, (((0,), (0,)), ((), ())), preferred_element_type=jnp.float32
    )
    center_grad = (first - correction).astype(jnp.bfloat16)
    return (predictions, center_grad, sub_increment)


def iota(shape, dim):
    return lax.broadcasted_iota(jnp.int32, shape, dim)


def to_col(row, n):
    return jnp.sum(jnp.where(iota((n, n), 0) == iota((n, n), 1), row, 0.0), axis=1, keepdims=True)


def to_row(col, n):
    return jnp.sum(jnp.where(iota((n, n), 0) == iota((n, n), 1), col, 0.0), axis=0, keepdims=True)


def hot(mask):
    return jnp.where(mask, 1.0, 0.0).astype(BF16)


def nn(a, b, **kw):
    return jnp.dot(a, b, preferred_element_type=F32, **kw)


def nt(a, b):
    return lax.dot_general(a, b, (((1,), (1,)), ((), ())), preferred_element_type=F32)


def tn(a, b):
    return lax.dot_general(a, b, (((0,), (0,)), ((), ())), preferred_element_type=F32)


def sq_col(rows):
    return jnp.sum(jnp.square(rows.astype(F32)), axis=1, keepdims=True)


def kern(left, right, left_sq, right_sq):
    dist = jnp.sqrt(jnp.maximum(left_sq + right_sq - 2.0 * nt(left, right), 0.0) + SOFTEN)
    return jnp.exp(-dist / SPREAD).astype(BF16)


def body(
    n_grid, chips, share, classes,
    centers, weights, batch_index, labels, sub_index, eigvecs, scales,
    pred_out, grad_out, sub_out,
    csib, wts, wsib, gath, gath2, batch, part, recv, pred, left, resid,
    c_sem, w_sem, g_send, g_fwd, g_recv, h_send, h_fwd, h_recv,
    p_send, p_fwd, p_recv, r_send, r_recv,
):
    held, width = centers.shape
    rows_b = batch_index.shape[1]
    cp = wts.shape[1]
    sub_dev, rank = eigvecs.shape
    n = chips * CORES
    subset = n * sub_dev
    half = rows_b // CORES
    me = lax.axis_index("blk") * n_grid + lax.axis_index("grid")
    chip, core = me // CORES, lax.rem(me, CORES)

    def at(dev):
        return (dev // n_grid, lax.rem(dev, n_grid))

    sib = chip * CORES + (1 - core)

    def peer_chip(k):
        return lax.rem(chip + k, chips)

    def from_chip(k):
        return lax.rem(chip + chips - k, chips)

    barrier = pltpu.get_barrier_semaphore()

    def greet(k, carry):
        pl.semaphore_signal(
            barrier, inc=1, device_id=at(peer_chip(k) * CORES + core), device_id_type=MESH
        )
        return carry

    pl.semaphore_signal(barrier, inc=1, device_id=at(sib), device_id_type=MESH)
    lax.fori_loop(1, chips, greet, 0)

    wts[...] = jnp.zeros_like(wts)
    wts[:, :classes] = weights[...].astype(BF16)

    bi_row = batch_index[...].astype(F32)
    bi_col = to_col(bi_row, rows_b)
    own_row = jnp.floor((bi_row + 0.5) * (1.0 / held))
    own_col = jnp.floor((bi_col + 0.5) * (1.0 / held))
    r_i, c_i = iota((rows_b, rows_b), 0), iota((rows_b, rows_b), 1)
    same = own_col == own_row
    rank_row = jnp.sum(jnp.where(same, jnp.where(r_i < c_i, 1.0, 0.0), 0.0), axis=0, keepdims=True)
    rank_col = jnp.sum(jnp.where(same, jnp.where(c_i < r_i, 1.0, 0.0), 0.0), axis=1, keepdims=True)
    pos_row = own_row * share + rank_row
    pos_col = own_col * share + rank_col
    mine = (iota((share, rows_b), 0) + me * share).astype(F32)
    within = bi_col - own_col * held
    pick = hot(within == iota((rows_b, held), 1).astype(F32))
    sel = nn(hot(mine == pos_row), pick).astype(BF16)
    gath[me] = nn(sel, centers[...]).astype(BF16)

    pair = 2 * sub_dev
    sub_col = jnp.sum(
        jnp.where(
            iota((pair, sub_dev), 0) == iota((pair, sub_dev), 1),
            sub_index[...].astype(F32), 0.0,
        ),
        axis=1, keepdims=True,
    )
    sub_hot = hot(
        (iota((pair, held), 0) < sub_dev) & (sub_col == iota((pair, held), 1).astype(F32))
    )
    eig16 = nn(
        hot(iota((pair, sub_dev), 0) == iota((pair, sub_dev), 1) + sub_dev), eigvecs[...]
    ).astype(BF16)
    eig16 = nn(eig16, hot(iota((rank, width), 0) == iota((rank, width), 1)))
    gath2[me] = (nn(sub_hot, centers[...]) + eig16).astype(BF16)

    pl.semaphore_wait(barrier, chips)

    def send(src, dst, s_sem, r_sem, dev):
        return pltpu.make_async_remote_copy(
            src_ref=src, dst_ref=dst, send_sem=s_sem, recv_sem=r_sem,
            device_id=at(dev), device_id_type=MESH,
        )

    def gather_start(buf, slot, s_sem, f_sem, r_sem):
        def go(k, carry):
            q = peer_chip(k)
            send(buf.at[slot(me)], buf.at[slot(me)], s_sem.at[q], r_sem.at[me],
                 q * CORES + core).start()
            return carry

        lax.fori_loop(1, chips, go, 0)
        send(buf.at[slot(me)], buf.at[slot(me)], f_sem.at[chip], r_sem.at[me], sib).start()

    def gather_pass(buf, slot, f_sem, r_sem):
        def go(k, carry):
            q = from_chip(k)
            dev = q * CORES + core
            here = buf.at[slot(dev)]
            send(here, here, f_sem.at[q], r_sem.at[dev], sib).wait_recv()
            send(here, here, f_sem.at[q], r_sem.at[dev], sib).start()
            return carry

        lax.fori_loop(1, chips, go, 0)

    def gather_rest(buf, slot, f_sem, r_sem):
        def go(q, carry):
            dev = q * CORES + (1 - core)
            here = buf.at[slot(dev)]
            send(here, here, f_sem.at[q], r_sem.at[dev], sib).wait_recv()
            return carry

        lax.fori_loop(0, chips, go, 0)

    def gather_end(buf, slot, s_sem, f_sem, r_sem):
        def go(k, carry):
            q = peer_chip(k)
            here = buf.at[slot(me)]
            send(here, here, s_sem.at[q], r_sem.at[me], sib).wait_send()
            there = buf.at[slot(q * CORES + core)]
            send(there, there, f_sem.at[q], r_sem.at[me], sib).wait_send()
            return carry

        lax.fori_loop(1, chips, go, 0)
        here = buf.at[slot(me)]
        send(here, here, f_sem.at[chip], r_sem.at[me], sib).wait_send()

    by_dev = lambda dev: dev
    by_row = lambda dev: lax.rem(dev, CORES) * chips + dev // CORES

    gather_start(gath, by_dev, g_send, g_fwd, g_recv)
    c_copy = send(centers, csib, c_sem.at[0], c_sem.at[1], sib)
    w_copy = send(wts, wsib, w_sem.at[0], w_sem.at[1], sib)
    c_copy.start()
    w_copy.start()
    gather_start(gath2, by_dev, h_send, h_fwd, h_recv)

    order = hot(pos_col == c_i.astype(F32))
    c_sq = sq_col(centers[...])
    c_sq_row = to_row(c_sq, held)
    lab_row = labels[...].astype(F32)
    lab_col = to_col(lab_row, rows_b)
    first = core * half + chip * share
    lab_here = jnp.sum(
        jnp.where(iota((share, rows_b), 0) + first == iota((share, rows_b), 1), lab_row, 0.0),
        axis=1, keepdims=True,
    )

    gather_pass(gath, by_dev, g_fwd, g_recv)
    gather_rest(gath, by_dev, g_fwd, g_recv)
    c_copy.wait_recv()
    w_copy.wait_recv()

    batch[...] = nn(order, gath[...].reshape(rows_b, width)).astype(BF16)
    s_sq_row = to_row(sq_col(csib[...]), held)
    rows = batch[pl.ds(pl.multiple_of(core * half, half), half), :]
    rows_sq = sq_col(rows)
    sums = nn(kern(rows, centers[...], rows_sq, c_sq_row), wts[...])
    sums = sums + nn(kern(rows, csib[...], rows_sq, s_sq_row), wsib[...])
    part[...] = sums.reshape(chips, share, cp)

    def scatter(k, carry):
        q = peer_chip(k)
        send(part.at[q], recv.at[chip], r_send.at[q], r_recv.at[chip], q * CORES + core).start()
        return carry

    lax.fori_loop(1, chips, scatter, 0)

    b_sq_row = to_row(sq_col(batch[...]), rows_b)
    gather_pass(gath2, by_dev, h_fwd, h_recv)
    kbz_t = kern(centers[...], batch[...], c_sq, b_sq_row).astype(F32)
    gather_rest(gath2, by_dev, h_fwd, h_recv)
    both = gath2[...].reshape(n * pair, width)
    s_i, g_i = iota((subset, n * pair), 0), iota((subset, n * pair), 1)
    spot = s_i + lax.div(s_i, sub_dev) * sub_dev
    sub_rows = nn(hot(spot == g_i), both).astype(BF16)
    vecs = nn(hot(spot + sub_dev == g_i), both).astype(BF16)[:, :rank]
    sub_sq = sq_col(sub_rows)
    kze = nn(kern(centers[...], sub_rows, c_sq, to_row(sub_sq, subset)), vecs)
    proj = tn(vecs, kern(sub_rows, batch[...], sub_sq, b_sq_row))
    to_grad = kbz_t - nn(kze * scales[...], proj, precision=HIGHEST)
    to_sub = nn(eigvecs[...].astype(F32) * scales[...], proj, precision=HIGHEST)
    high = to_grad.astype(BF16)
    left[:held, :] = high
    left[held:2 * held, :] = (to_grad - high.astype(F32)).astype(BF16)
    sub_high = to_sub.astype(BF16).astype(F32)
    left[2 * held:, :] = jnp.concatenate([sub_high, to_sub - sub_high], axis=0).astype(BF16)

    total = part[chip]
    for k in range(1, chips):
        q = from_chip(k)
        send(part.at[q], recv.at[q], r_send.at[q], r_recv.at[q], sib).wait_recv()
        total = total + recv[q]
    lanes = iota((share, cp), 1)
    at_label = jnp.sum(
        jnp.where(lanes.astype(F32) == lab_here, total - 1.0, 0.0), axis=1, keepdims=True
    )
    pred[by_row(me)] = jnp.where(lanes == classes, at_label, total).astype(BF16)

    gather_start(pred, by_row, p_send, p_fwd, p_recv)
    gather_pass(pred, by_row, p_fwd, p_recv)
    gather_rest(pred, by_row, p_fwd, p_recv)

    block = 128
    for r in range(0, rows_b, block):
        held_pred = pred[r // share:(r + block) // share].reshape(block, cp)
        pred_out[r:r + block, :] = held_pred[:, :classes]
        value = held_pred.astype(F32)
        lanes = iota((block, cp), 1)
        fix = jnp.sum(jnp.where(lanes == classes, value, 0.0), axis=1, keepdims=True)
        resid[r:r + block, :] = jnp.where(
            lanes.astype(F32) == lab_col[r:r + block], fix, value
        ).astype(BF16)
    out = nn(left[...], resid[...])
    grad_out[...] = (out[:held] + out[held:2 * held]).astype(BF16)[:, :classes]
    sub_out[...] = (out[2 * held:2 * held + sub_dev] + out[2 * held + sub_dev:])[:, :classes]

    gather_end(gath, by_dev, g_send, g_fwd, g_recv)
    gather_end(gath2, by_dev, h_send, h_fwd, h_recv)
    gather_end(pred, by_row, p_send, p_fwd, p_recv)
    c_copy.wait_send()
    w_copy.wait_send()

    def sent(k, carry):
        q = peer_chip(k)
        send(part.at[q], recv.at[chip], r_send.at[q], r_recv.at[chip], sib).wait_send()
        return carry

    lax.fori_loop(1, chips, sent, 0)


def fused(n_blk, n_grid, centers, weights, batch_index, labels, sub_index, eigvecs, scales):
    n = n_blk * n_grid
    chips = n // CORES
    held, width = centers.shape
    classes = weights.shape[1]
    rows_b = batch_index.shape[0]
    sub_dev, rank = eigvecs.shape
    share = rows_b // n
    cp = pl.cdiv(classes + 1, 128) * 128
    dma = pltpu.SemaphoreType.DMA
    vmem = pl.BlockSpec(memory_space=pltpu.VMEM)
    return pl.pallas_call(
        functools.partial(body, n_grid, chips, share, classes),
        out_shape=(
            jax.ShapeDtypeStruct((rows_b, classes), BF16),
            jax.ShapeDtypeStruct((held, classes), BF16),
            jax.ShapeDtypeStruct((sub_dev, classes), F32),
        ),
        in_specs=[vmem] * 7,
        out_specs=(vmem, vmem, vmem),
        scratch_shapes=[
            pltpu.VMEM((held, width), BF16),
            pltpu.VMEM((held, cp), BF16),
            pltpu.VMEM((held, cp), BF16),
            pltpu.VMEM((n, share, width), BF16),
            pltpu.VMEM((n, 2 * sub_dev, width), BF16),
            pltpu.VMEM((rows_b, width), BF16),
            pltpu.VMEM((chips, share, cp), F32),
            pltpu.VMEM((chips, share, cp), F32),
            pltpu.VMEM((n, share, cp), BF16),
            pltpu.VMEM((2 * held + 2 * sub_dev, rows_b), BF16),
            pltpu.VMEM((rows_b, cp), BF16),
            dma((2,)), dma((2,)),
            dma((chips,)), dma((chips,)), dma((n,)),
            dma((chips,)), dma((chips,)), dma((n,)),
            dma((chips,)), dma((chips,)), dma((n,)),
            dma((chips,)), dma((chips,)),
        ],
        compiler_params=pltpu.CompilerParams(
            collective_id=0, has_side_effects=True, vmem_limit_bytes=48 * 1024 * 1024
        ),
    )(
        centers, weights, batch_index.reshape(1, rows_b), labels.reshape(1, rows_b),
        sub_index.reshape(1, sub_dev), eigvecs, scales.reshape(1, rank),
    )


def solution(mesh):
    n_blk, n_grid = mesh.shape["blk"], mesh.shape["grid"]
    n = n_blk * n_grid

    def step(centers, *rest):
        rows_b, sub_dev = rest[1].shape[0], rest[4].shape[0]
        whole_tiles = n_grid % CORES == 0 and rows_b % (16 * n) == 0 and sub_dev % 8 == 0
        if whole_tiles:
            return fused(n_blk, n_grid, centers, *rest)
        return local(centers, *rest)

    return jax.shard_map(
        step,
        mesh=mesh,
        in_specs=(
            P(("blk", "grid"), None),
            P(("blk", "grid"), None),
            P(),
            P(),
            P(("blk", "grid")),
            P(("blk", "grid"), None),
            P(),
        ),
        out_specs=(P(), P(("blk", "grid"), None), P(("blk", "grid"), None)),
        check_vma=False,
    )
```

```python
import functools

import jax
import jax.numpy as jnp
from jax import lax
from jax.experimental import pallas as pl
from jax.experimental.pallas import tpu as pltpu
from jax.sharding import PartitionSpec as P

SOFTEN = 1.0
SPREAD = 4.0
CORES = 2
MESH = pl.DeviceIdType.MESH
F32 = jnp.float32
BF16 = jnp.bfloat16
HIGHEST = lax.Precision.HIGHEST


def kernel(left, right):
    left_sq = jnp.sum(jnp.square(left.astype(jnp.float32)), axis=1)
    right_sq = jnp.sum(jnp.square(right.astype(jnp.float32)), axis=1)
    cross = lax.dot_general(
        left, right, (((1,), (1,)), ((), ())), preferred_element_type=jnp.float32
    )
    dist = jnp.sqrt(jnp.maximum(left_sq[:, None] + right_sq[None, :] - 2.0 * cross, 0.0) + SOFTEN)
    return jnp.exp(-dist / SPREAD)


def one_hot(label_rows, classes):
    return (label_rows[:, None] == jnp.arange(classes, dtype=jnp.int32)[None, :]).astype(
        jnp.float32
    )


def local(centers, weights, batch_index, labels, sub_index, eigvecs, scales):
    myself = lax.axis_index(("blk", "grid"))
    held = centers.shape[0]
    classes = weights.shape[1]
    owner = batch_index // held
    within = batch_index % held
    picked = jnp.take(centers, within, axis=0).astype(jnp.float32)
    picked = jnp.where((owner == myself)[:, None], picked, 0.0)
    batch = lax.psum(picked, ("blk", "grid")).astype(jnp.bfloat16)
    kbz = kernel(batch, centers).astype(jnp.bfloat16)
    partial_out = jnp.dot(kbz, weights.astype(jnp.bfloat16), preferred_element_type=jnp.float32)
    total = lax.psum(partial_out, ("blk", "grid"))
    predictions = total.astype(jnp.bfloat16)
    resid = (total - one_hot(labels, classes)).astype(jnp.bfloat16)
    subset_here = jnp.take(centers, sub_index, axis=0)
    sub_rows = lax.all_gather(subset_here, ("blk", "grid"), axis=0, tiled=True)
    vec_rows = lax.all_gather(eigvecs, ("blk", "grid"), axis=0, tiled=True)
    kzs = kernel(centers, sub_rows).astype(jnp.bfloat16)
    ksb_piece = kernel(sub_rows, batch).astype(jnp.bfloat16)
    kze_next = jnp.dot(kzs, vec_rows, preferred_element_type=jnp.float32)
    proj_next = lax.dot_general(
        vec_rows, ksb_piece, (((0,), (0,)), ((), ())), preferred_element_type=jnp.float32
    )
    coeff = jnp.dot(proj_next, resid.astype(jnp.float32), precision=lax.Precision.HIGHEST)
    scaled = scales[:, None] * coeff
    sub_increment = jnp.dot(eigvecs.astype(jnp.float32), scaled, precision=lax.Precision.HIGHEST)
    correction = jnp.dot(kze_next, scaled, precision=lax.Precision.HIGHEST)
    first = lax.dot_general(
        kbz, resid, (((0,), (0,)), ((), ())), preferred_element_type=jnp.float32
    )
    center_grad = (first - correction).astype(jnp.bfloat16)
    return (predictions, center_grad, sub_increment)


def iota(shape, dim):
    return lax.broadcasted_iota(jnp.int32, shape, dim)


def to_col(row, n):
    return jnp.sum(jnp.where(iota((n, n), 0) == iota((n, n), 1), row, 0.0), axis=1, keepdims=True)


def to_row(col, n):
    return jnp.sum(jnp.where(iota((n, n), 0) == iota((n, n), 1), col, 0.0), axis=0, keepdims=True)


def hot(mask):
    return jnp.where(mask, 1.0, 0.0).astype(BF16)


def nn(a, b, **kw):
    return jnp.dot(a, b, preferred_element_type=F32, **kw)


def nt(a, b):
    return lax.dot_general(a, b, (((1,), (1,)), ((), ())), preferred_element_type=F32)


def tn(a, b):
    return lax.dot_general(a, b, (((0,), (0,)), ((), ())), preferred_element_type=F32)


def sq_col(rows):
    return jnp.sum(jnp.square(rows.astype(F32)), axis=1, keepdims=True)


def kern(left, right, left_sq, right_sq):
    dist = jnp.sqrt(jnp.maximum(left_sq + right_sq - 2.0 * nt(left, right), 0.0) + SOFTEN)
    return jnp.exp(-dist / SPREAD).astype(BF16)


def body(
    n_blk, n_grid, share,
    centers, weights_t, batch_index, labels, sub_index, eigvecs, scales,
    pred_out, grad_out, sub_out,
    cbuf, wts, wbuf, gath, gath2, batch, part, recv, pred, fix, left, resid,
    c_send, c_fwd, c_recv, w_send, w_fwd, w_recv, g_send, g_fwd, g_recv, h_send, h_fwd, h_recv,
    pz_send, pp_send, ps_send, p_recv, r_send, r_recv,
):
    held, width = centers.shape
    classes = weights_t.shape[0]
    rows_b = batch_index.shape[1]
    gc, cs, _ = wts.shape
    nz, rz, _ = part.shape
    cp = gc * cs
    sub_dev, rank = eigvecs.shape
    n = n_blk * n_grid
    chips = n // CORES
    subset = n * sub_dev
    half = rows_b // CORES
    blk, grid = lax.axis_index("blk"), lax.axis_index("grid")
    me = blk * n_grid + grid
    chip, core = me // CORES, lax.rem(me, CORES)
    z, j = grid // (2 * CORES), blk * 2 + lax.rem(grid // CORES, 2)

    def at(dev):
        return (dev // n_grid, lax.rem(dev, n_grid))

    def dev_of(pj, pz, pc):
        return (pj // 2) * n_grid + pz * 2 * CORES + lax.rem(pj, 2) * CORES + pc

    sib = chip * CORES + (1 - core)

    def peer_chip(k):
        return lax.rem(chip + k, chips)

    def from_chip(k):
        return lax.rem(chip + chips - k, chips)

    barrier = pltpu.get_barrier_semaphore()

    def greet(k, carry):
        pl.semaphore_signal(
            barrier, inc=1, device_id=at(peer_chip(k) * CORES + core), device_id_type=MESH
        )
        return carry

    pl.semaphore_signal(barrier, inc=1, device_id=at(sib), device_id_type=MESH)
    lax.fori_loop(1, chips, greet, 0)

    bi_row = batch_index[...].astype(F32)
    bi_col = to_col(bi_row, rows_b)
    own_row = jnp.floor((bi_row + 0.5) * (1.0 / held))
    own_col = jnp.floor((bi_col + 0.5) * (1.0 / held))
    r_i, c_i = iota((rows_b, rows_b), 0), iota((rows_b, rows_b), 1)
    same = own_col == own_row
    rank_row = jnp.sum(jnp.where(same, jnp.where(r_i < c_i, 1.0, 0.0), 0.0), axis=0, keepdims=True)
    pos_row = own_row * share + rank_row
    mine = (iota((share, rows_b), 0) + me * share).astype(F32)
    within = bi_col - own_col * held
    pick = hot(within == iota((rows_b, held), 1).astype(F32))
    sel = nn(hot(mine == pos_row), pick).astype(BF16)
    gath[me] = nn(sel, centers[...]).astype(BF16)

    per = cs
    for q in range(gc):
        lo, hi = q * per, min((q + 1) * per, classes)
        if hi - lo < cs:
            wts[q] = jnp.zeros((cs, held), BF16)
        if hi > lo:
            wts[q, :hi - lo, :] = weights_t[lo:hi, :].astype(BF16)

    pair = 2 * sub_dev
    sub_col = jnp.sum(
        jnp.where(
            iota((pair, sub_dev), 0) == iota((pair, sub_dev), 1),
            sub_index[...].astype(F32), 0.0,
        ),
        axis=1, keepdims=True,
    )
    sub_hot = hot(
        (iota((pair, held), 0) < sub_dev) & (sub_col == iota((pair, held), 1).astype(F32))
    )
    eig16 = nn(
        hot(iota((pair, sub_dev), 0) == iota((pair, sub_dev), 1) + sub_dev), eigvecs[...]
    ).astype(BF16)
    eig16 = nn(eig16, hot(iota((rank, width), 0) == iota((rank, width), 1)))
    gath2[me] = (nn(sub_hot, centers[...]) + eig16).astype(BF16)

    pl.semaphore_wait(barrier, chips)

    def send(src, dst, s_sem, r_sem, dev):
        return pltpu.make_async_remote_copy(
            src_ref=src, dst_ref=dst, send_sem=s_sem, recv_sem=r_sem,
            device_id=at(dev), device_id_type=MESH,
        )

    def gather_start(buf, s_sem, f_sem, r_sem):
        def go(k, carry):
            q = peer_chip(k)
            send(buf.at[me], buf.at[me], s_sem.at[q], r_sem.at[me], q * CORES + core).start()
            return carry

        lax.fori_loop(1, chips, go, 0)
        send(buf.at[me], buf.at[me], f_sem.at[chip], r_sem.at[me], sib).start()

    def gather_pass(buf, f_sem, r_sem):
        def go(k, carry):
            q = from_chip(k)
            dev = q * CORES + core
            send(buf.at[dev], buf.at[dev], f_sem.at[q], r_sem.at[dev], sib).wait_recv()
            send(buf.at[dev], buf.at[dev], f_sem.at[q], r_sem.at[dev], sib).start()
            return carry

        lax.fori_loop(1, chips, go, 0)

    def gather_rest(buf, f_sem, r_sem):
        def go(q, carry):
            dev = q * CORES + (1 - core)
            send(buf.at[dev], buf.at[dev], f_sem.at[q], r_sem.at[dev], sib).wait_recv()
            return carry

        lax.fori_loop(0, chips, go, 0)

    def gather_end(buf, s_sem, f_sem, r_sem):
        def go(k, carry):
            q = peer_chip(k)
            send(buf.at[me], buf.at[me], s_sem.at[q], r_sem.at[me], sib).wait_send()
            dev = q * CORES + core
            send(buf.at[dev], buf.at[dev], f_sem.at[q], r_sem.at[me], sib).wait_send()
            return carry

        lax.fori_loop(1, chips, go, 0)
        send(buf.at[me], buf.at[me], f_sem.at[chip], r_sem.at[me], sib).wait_send()

    gather_start(gath, g_send, g_fwd, g_recv)

    own = j * CORES + core
    other = j * CORES + (1 - core)

    def c_direct(q):
        return send(centers, cbuf.at[own], c_send.at[q], c_recv.at[own], dev_of(q, z, core))

    def w_direct(q):
        return send(wts.at[q], wbuf.at[own], w_send.at[q], w_recv.at[own], dev_of(q, z, core))

    def c_pass(q):
        slot = q * CORES + core
        return send(cbuf.at[slot], cbuf.at[slot], c_fwd.at[q], c_recv.at[slot], sib)

    def w_pass(q):
        slot = q * CORES + core
        return send(wbuf.at[slot], wbuf.at[slot], w_fwd.at[q], w_recv.at[slot], sib)

    c_own = send(centers, cbuf.at[own], c_send.at[j], c_recv.at[own], sib)
    w_own = send(wts.at[j], wbuf.at[own], w_send.at[j], w_recv.at[own], sib)
    c_own.start()
    w_own.start()
    near = [lax.rem(j + k, gc) for k in range(1, gc)]
    for q in near:
        c_direct(q).start()
        w_direct(q).start()
    gather_start(gath2, h_send, h_fwd, h_recv)

    rank_col = jnp.sum(jnp.where(same, jnp.where(c_i < r_i, 1.0, 0.0), 0.0), axis=1, keepdims=True)
    pos_col = own_col * share + rank_col
    order = hot(pos_col == c_i.astype(F32))
    c_sq = sq_col(centers[...])
    c_sq_row = to_row(c_sq, held)
    lab_row = labels[...].astype(F32)
    lab_col = to_col(lab_row, rows_b)
    first = core * half + z * rz
    lab_here = jnp.sum(
        jnp.where(iota((rz, rows_b), 0) + first == iota((rz, rows_b), 1), lab_row, 0.0),
        axis=1, keepdims=True,
    )

    gather_pass(gath, g_fwd, g_recv)
    gather_rest(gath, g_fwd, g_recv)

    batch[...] = nn(order, gath[...].reshape(rows_b, width)).astype(BF16)
    rows = batch[pl.ds(pl.multiple_of(core * half, half), half), :]
    rows_sq = sq_col(rows)

    def add_from(slot):
        there = cbuf[slot]
        there_sq = to_row(sq_col(there), held)
        return nt(kern(rows, there, rows_sq, there_sq), wbuf[slot])

    part[...] = nt(kern(rows, centers[...], rows_sq, c_sq_row), wts[j]).reshape(nz, rz, cs)
    send(cbuf.at[other], cbuf.at[other], c_fwd.at[j], c_recv.at[other], sib).wait_recv()
    send(wbuf.at[other], wbuf.at[other], w_fwd.at[j], w_recv.at[other], sib).wait_recv()
    part[...] += add_from(other).reshape(nz, rz, cs)
    for q in near[::-1]:
        c_pass(q).wait_recv()
        c_pass(q).start()
        w_pass(q).wait_recv()
        w_pass(q).start()
        part[...] += add_from(q * CORES + core).reshape(nz, rz, cs)
    for q in near[::-1]:
        slot = q * CORES + 1 - core
        send(cbuf.at[slot], cbuf.at[slot], c_fwd.at[q], c_recv.at[slot], sib).wait_recv()
        send(wbuf.at[slot], wbuf.at[slot], w_fwd.at[q], w_recv.at[slot], sib).wait_recv()
        part[...] += add_from(slot).reshape(nz, rz, cs)

    def sum_copy(q):
        return send(part.at[q], recv.at[z], r_send.at[q], r_recv.at[z], dev_of(j, q, core))

    along = [lax.rem(z + k, nz) for k in range(1, nz)]
    for q in along:
        sum_copy(q).start()

    b_sq_row = to_row(sq_col(batch[...]), rows_b)
    gather_pass(gath2, h_fwd, h_recv)
    kbz_t = kern(centers[...], batch[...], c_sq, b_sq_row).astype(F32)
    gather_rest(gath2, h_fwd, h_recv)
    both = gath2[...].reshape(n * pair, width)
    s_i, g_i = iota((subset, n * pair), 0), iota((subset, n * pair), 1)
    spot = s_i + lax.div(s_i, sub_dev) * sub_dev
    sub_rows = nn(hot(spot == g_i), both).astype(BF16)
    vecs = nn(hot(spot + sub_dev == g_i), both).astype(BF16)[:, :rank]
    sub_sq = sq_col(sub_rows)
    kze = nn(kern(centers[...], sub_rows, c_sq, to_row(sub_sq, subset)), vecs)
    proj = tn(vecs, kern(sub_rows, batch[...], sub_sq, b_sq_row))
    to_grad = kbz_t - nn(kze * scales[...], proj, precision=HIGHEST)
    to_sub = nn(eigvecs[...].astype(F32) * scales[...], proj, precision=HIGHEST)
    high = to_grad.astype(BF16)
    left[:held, :] = high
    left[held:2 * held, :] = (to_grad - high.astype(F32)).astype(BF16)
    sub_high = to_sub.astype(BF16).astype(F32)
    left[2 * held:, :] = jnp.concatenate([sub_high, to_sub - sub_high], axis=0).astype(BF16)

    total = part[z]
    for q in along[::-1]:
        send(part.at[q], recv.at[q], r_send.at[q], r_recv.at[q], sib).wait_recv()
        total = total + recv[q]
    lanes = iota((rz, cs), 1) + j * cs
    at_label = jnp.sum(
        jnp.where(lanes.astype(F32) == lab_here, total - 1.0, 0.0), axis=1, keepdims=True
    )
    spread = jnp.sum(
        jnp.where(iota((rz, 128), 0) == iota((rz, 128), 1), at_label, 0.0), axis=0, keepdims=True
    )
    cols = pl.ds(pl.multiple_of(j * cs, 128), cs)
    pred[core * nz + z, :, cols] = total.astype(BF16)
    fix[me] = jnp.broadcast_to(spread, (16, 128)).astype(BF16)

    def piece(t, pj, pz, pc):
        if t == 0:
            return pred.at[pc * nz + pz, :, pl.ds(pl.multiple_of(pj * cs, 128), cs)]
        return fix.at[dev_of(pj, pz, pc)]

    def pass_on(t, pj, pz, s_sem, dev):
        here = piece(t, pj, pz, core)
        return send(here, here, s_sem, p_recv.at[t, dev_of(pj, pz, core)], dev)

    def to_z(t, q):
        return pass_on(t, j, z, pz_send.at[t, q], dev_of(j, q, core))

    def to_plane(t, pz, q):
        return pass_on(t, j, pz, pp_send.at[t, pz * gc + q], dev_of(q, z, core))

    def to_sib(t, pj, pz):
        return pass_on(t, pj, pz, ps_send.at[t, pz * gc + pj], sib)

    def arrived(t, pj, pz, pc):
        here = piece(t, pj, pz, pc)
        return send(here, here, ps_send.at[t, pz * gc + pj], p_recv.at[t, dev_of(pj, pz, pc)], sib)

    for t in range(2):
        for q in along:
            to_z(t, q).start()
    for t in range(2):
        for q in near:
            to_plane(t, z, q).start()
        to_sib(t, j, z).start()
    for pz in along[::-1]:
        for t in range(2):
            arrived(t, j, pz, core).wait_recv()
            for q in near:
                to_plane(t, pz, q).start()
            to_sib(t, j, pz).start()
    for pz in [z] + along[::-1]:
        for q in near[::-1]:
            for t in range(2):
                arrived(t, q, pz, core).wait_recv()
                to_sib(t, q, pz).start()
    for pz in [z] + along[::-1]:
        for q in [j] + near[::-1]:
            for t in range(2):
                arrived(t, q, pz, 1 - core).wait_recv()

    for r in range(CORES * nz):
        held_pred = pred[r]
        lo = r * rz
        pred_out[lo:lo + rz, :] = held_pred[:, :classes]
        value = held_pred.astype(F32)
        fixes = jnp.zeros((16, 128), F32)
        for q in range(gc):
            fixes = fixes + fix[dev_of(q, r % nz, r // nz)].astype(F32)
        fix_col = jnp.sum(
            jnp.where(iota((rz, 128), 0) == iota((rz, 128), 1), fixes[:1], 0.0),
            axis=1, keepdims=True,
        )
        resid[lo:lo + rz, :] = jnp.where(
            iota((rz, cp), 1).astype(F32) == lab_col[lo:lo + rz], fix_col, value
        ).astype(BF16)
    out = nn(left[...], resid[...])
    grad_out[...] = (out[:held] + out[held:2 * held]).astype(BF16)[:, :classes]
    sub_out[...] = (out[2 * held:2 * held + sub_dev] + out[2 * held + sub_dev:])[:, :classes]

    gather_end(gath, g_send, g_fwd, g_recv)
    gather_end(gath2, h_send, h_fwd, h_recv)
    c_own.wait_send()
    w_own.wait_send()
    for q in near:
        c_direct(q).wait_send()
        w_direct(q).wait_send()
        c_pass(q).wait_send()
        w_pass(q).wait_send()
    for q in along:
        sum_copy(q).wait_send()
    for t in range(2):
        for q in along:
            to_z(t, q).wait_send()
        for pz in [z] + along:
            for q in near:
                to_plane(t, pz, q).wait_send()
            for q in [j] + near:
                to_sib(t, q, pz).wait_send()


def fused(n_blk, n_grid, centers, weights, batch_index, labels, sub_index, eigvecs, scales):
    n = n_blk * n_grid
    chips = n // CORES
    held, width = centers.shape
    classes = weights.shape[1]
    rows_b = batch_index.shape[0]
    sub_dev, rank = eigvecs.shape
    share = rows_b // n
    gc, nz = n_blk * 2, n_grid // (2 * CORES)
    cs = pl.cdiv(classes, gc * 128) * 128
    rz = rows_b // (CORES * nz)
    dma = pltpu.SemaphoreType.DMA
    vmem = pl.BlockSpec(memory_space=pltpu.VMEM)
    return pl.pallas_call(
        functools.partial(body, n_blk, n_grid, share),
        out_shape=(
            jax.ShapeDtypeStruct((rows_b, classes), BF16),
            jax.ShapeDtypeStruct((held, classes), BF16),
            jax.ShapeDtypeStruct((sub_dev, classes), F32),
        ),
        in_specs=[vmem] * 7,
        out_specs=(vmem, vmem, vmem),
        scratch_shapes=[
            pltpu.VMEM((gc * CORES, held, width), BF16),
            pltpu.VMEM((gc, cs, held), BF16),
            pltpu.VMEM((gc * CORES, cs, held), BF16),
            pltpu.VMEM((n, share, width), BF16),
            pltpu.VMEM((n, 2 * sub_dev, width), BF16),
            pltpu.VMEM((rows_b, width), BF16),
            pltpu.VMEM((nz, rz, cs), F32),
            pltpu.VMEM((nz, rz, cs), F32),
            pltpu.VMEM((CORES * nz, rz, gc * cs), BF16),
            pltpu.VMEM((n, 16, 128), BF16),
            pltpu.VMEM((2 * held + 2 * sub_dev, rows_b), BF16),
            pltpu.VMEM((rows_b, gc * cs), BF16),
            dma((gc,)), dma((gc,)), dma((gc * CORES,)),
            dma((gc,)), dma((gc,)), dma((gc * CORES,)),
            dma((chips,)), dma((chips,)), dma((n,)),
            dma((chips,)), dma((chips,)), dma((n,)),
            dma((2, nz)), dma((2, nz * gc)), dma((2, nz * gc)), dma((2, n)),
            dma((nz,)), dma((nz,)),
        ],
        compiler_params=pltpu.CompilerParams(
            collective_id=0, has_side_effects=True, vmem_limit_bytes=48 * 1024 * 1024
        ),
    )(
        centers, weights.T, batch_index.reshape(1, rows_b), labels.reshape(1, rows_b),
        sub_index.reshape(1, sub_dev), eigvecs, scales.reshape(1, rank),
    )


def solution(mesh):
    n_blk, n_grid = mesh.shape["blk"], mesh.shape["grid"]
    n = n_blk * n_grid

    def step(centers, *rest):
        rows_b, sub_dev = rest[1].shape[0], rest[4].shape[0]
        nz = n_grid // (2 * CORES)
        whole_tiles = (
            n_grid % (2 * CORES) == 0 and rows_b % (16 * n) == 0 and sub_dev % 8 == 0
            and rows_b <= 128 * CORES * nz
        )
        if whole_tiles:
            return fused(n_blk, n_grid, centers, *rest)
        return local(centers, *rest)

    return jax.shard_map(
        step,
        mesh=mesh,
        in_specs=(
            P(("blk", "grid"), None),
            P(("blk", "grid"), None),
            P(),
            P(),
            P(("blk", "grid")),
            P(("blk", "grid"), None),
            P(),
        ),
        out_specs=(P(), P(("blk", "grid"), None), P(("blk", "grid"), None)),
        check_vma=False,
    )
```

```python
import functools

import jax
import jax.numpy as jnp
from jax import lax
from jax.experimental import pallas as pl
from jax.experimental.pallas import tpu as pltpu
from jax.sharding import PartitionSpec as P

SOFTEN = 1.0
SPREAD = 4.0
CORES = 2
MESH = pl.DeviceIdType.MESH
F32 = jnp.float32
BF16 = jnp.bfloat16
HIGHEST = lax.Precision.HIGHEST


def kernel(left, right):
    left_sq = jnp.sum(jnp.square(left.astype(jnp.float32)), axis=1)
    right_sq = jnp.sum(jnp.square(right.astype(jnp.float32)), axis=1)
    cross = lax.dot_general(
        left, right, (((1,), (1,)), ((), ())), preferred_element_type=jnp.float32
    )
    dist = jnp.sqrt(jnp.maximum(left_sq[:, None] + right_sq[None, :] - 2.0 * cross, 0.0) + SOFTEN)
    return jnp.exp(-dist / SPREAD)


def one_hot(label_rows, classes):
    return (label_rows[:, None] == jnp.arange(classes, dtype=jnp.int32)[None, :]).astype(
        jnp.float32
    )


def local(centers, weights, batch_index, labels, sub_index, eigvecs, scales):
    myself = lax.axis_index(("blk", "grid"))
    held = centers.shape[0]
    classes = weights.shape[1]
    owner = batch_index // held
    within = batch_index % held
    picked = jnp.take(centers, within, axis=0).astype(jnp.float32)
    picked = jnp.where((owner == myself)[:, None], picked, 0.0)
    batch = lax.psum(picked, ("blk", "grid")).astype(jnp.bfloat16)
    kbz = kernel(batch, centers).astype(jnp.bfloat16)
    partial_out = jnp.dot(kbz, weights.astype(jnp.bfloat16), preferred_element_type=jnp.float32)
    total = lax.psum(partial_out, ("blk", "grid"))
    predictions = total.astype(jnp.bfloat16)
    resid = (total - one_hot(labels, classes)).astype(jnp.bfloat16)
    subset_here = jnp.take(centers, sub_index, axis=0)
    sub_rows = lax.all_gather(subset_here, ("blk", "grid"), axis=0, tiled=True)
    vec_rows = lax.all_gather(eigvecs, ("blk", "grid"), axis=0, tiled=True)
    kzs = kernel(centers, sub_rows).astype(jnp.bfloat16)
    ksb_piece = kernel(sub_rows, batch).astype(jnp.bfloat16)
    kze_next = jnp.dot(kzs, vec_rows, preferred_element_type=jnp.float32)
    proj_next = lax.dot_general(
        vec_rows, ksb_piece, (((0,), (0,)), ((), ())), preferred_element_type=jnp.float32
    )
    coeff = jnp.dot(proj_next, resid.astype(jnp.float32), precision=lax.Precision.HIGHEST)
    scaled = scales[:, None] * coeff
    sub_increment = jnp.dot(eigvecs.astype(jnp.float32), scaled, precision=lax.Precision.HIGHEST)
    correction = jnp.dot(kze_next, scaled, precision=lax.Precision.HIGHEST)
    first = lax.dot_general(
        kbz, resid, (((0,), (0,)), ((), ())), preferred_element_type=jnp.float32
    )
    center_grad = (first - correction).astype(jnp.bfloat16)
    return (predictions, center_grad, sub_increment)


def iota(shape, dim):
    return lax.broadcasted_iota(jnp.int32, shape, dim)


def to_col(row, n):
    return jnp.sum(jnp.where(iota((n, n), 0) == iota((n, n), 1), row, 0.0), axis=1, keepdims=True)


def to_row(col, n):
    return jnp.sum(jnp.where(iota((n, n), 0) == iota((n, n), 1), col, 0.0), axis=0, keepdims=True)


def hot(mask):
    return jnp.where(mask, 1.0, 0.0).astype(BF16)


def nn(a, b, **kw):
    return jnp.dot(a, b, preferred_element_type=F32, **kw)


def nt(a, b):
    return lax.dot_general(a, b, (((1,), (1,)), ((), ())), preferred_element_type=F32)


def tn(a, b):
    return lax.dot_general(a, b, (((0,), (0,)), ((), ())), preferred_element_type=F32)


def sq_col(rows):
    return jnp.sum(jnp.square(rows.astype(F32)), axis=1, keepdims=True)


def kern(left, right, left_sq, right_sq):
    dist = jnp.sqrt(jnp.maximum(left_sq + right_sq - 2.0 * nt(left, right), 0.0) + SOFTEN)
    return jnp.exp(-dist / SPREAD).astype(BF16)


def body(
    n_blk, n_grid, share,
    centers, weights_t, batch_index, labels, sub_index, eigvecs, scales,
    pred_out, grad_out, sub_out,
    cbuf, wts, wbuf, gath, gath2, batch, part, recv, pred, fix, left, resid, lab_buf,
    c_send, c_fwd, c_recv, w_send, w_fwd, w_recv, g_send, g_fwd, g_recv, h_send, h_fwd, h_recv,
    pz_send, pp_send, ps_send, p_recv, r_send, r_recv,
):
    held, width = centers.shape
    classes = weights_t.shape[0]
    rows_b = batch_index.shape[1]
    gc, cs, _ = wts.shape
    nz, rz, _ = part.shape
    cp = gc * cs
    sub_dev, rank = eigvecs.shape
    n = n_blk * n_grid
    chips = n // CORES
    subset = n * sub_dev
    half = rows_b // CORES
    blk, grid = lax.axis_index("blk"), lax.axis_index("grid")
    me = blk * n_grid + grid
    chip, core = me // CORES, lax.rem(me, CORES)
    z, j = grid // (2 * CORES), blk * 2 + lax.rem(grid // CORES, 2)

    def at(dev):
        return (dev // n_grid, lax.rem(dev, n_grid))

    def dev_of(pj, pz, pc):
        return (pj // 2) * n_grid + pz * 2 * CORES + lax.rem(pj, 2) * CORES + pc

    sib = chip * CORES + (1 - core)

    def peer_chip(k):
        return lax.rem(chip + k, chips)

    def from_chip(k):
        return lax.rem(chip + chips - k, chips)

    barrier = pltpu.get_barrier_semaphore()

    def greet(k, carry):
        pl.semaphore_signal(
            barrier, inc=1, device_id=at(peer_chip(k) * CORES + core), device_id_type=MESH
        )
        return carry

    pl.semaphore_signal(barrier, inc=1, device_id=at(sib), device_id_type=MESH)
    lax.fori_loop(1, chips, greet, 0)

    bi_row = batch_index[...].astype(F32)
    own_row = jnp.floor((bi_row + 0.5) * (1.0 / held))
    r_i, c_i = iota((rows_b, rows_b), 0), iota((rows_b, rows_b), 1)
    here_row = jnp.broadcast_to(jnp.where(own_row == me.astype(F32), 1.0, 0.0), (16, rows_b))
    ahead = nn(here_row.astype(BF16), hot(r_i < c_i))[:1]
    nth = jnp.where(own_row == me.astype(F32), ahead, -1.0)
    within = bi_row - own_row * held
    pick = hot(iota((held, rows_b), 0).astype(F32) == within)
    sel = nt(hot(iota((share, rows_b), 0).astype(F32) == nth), pick).astype(BF16)
    gath[me] = nn(sel, centers[...]).astype(BF16)

    per = cs
    for q in range(gc):
        lo, hi = q * per, min((q + 1) * per, classes)
        if hi - lo < cs:
            wts[q] = jnp.zeros((cs, held), BF16)
        if hi > lo:
            wts[q, :hi - lo, :] = weights_t[lo:hi, :].astype(BF16)

    pl.semaphore_wait(barrier, chips)

    def send(src, dst, s_sem, r_sem, dev):
        return pltpu.make_async_remote_copy(
            src_ref=src, dst_ref=dst, send_sem=s_sem, recv_sem=r_sem,
            device_id=at(dev), device_id_type=MESH,
        )

    def gather_start(buf, s_sem, f_sem, r_sem):
        def go(k, carry):
            q = peer_chip(k)
            send(buf.at[me], buf.at[me], s_sem.at[q], r_sem.at[me], q * CORES + core).start()
            return carry

        lax.fori_loop(1, chips, go, 0)
        send(buf.at[me], buf.at[me], f_sem.at[chip], r_sem.at[me], sib).start()

    def gather_pass(buf, f_sem, r_sem):
        def go(k, carry):
            q = from_chip(k)
            dev = q * CORES + core
            send(buf.at[dev], buf.at[dev], f_sem.at[q], r_sem.at[dev], sib).wait_recv()
            send(buf.at[dev], buf.at[dev], f_sem.at[q], r_sem.at[dev], sib).start()
            return carry

        lax.fori_loop(1, chips, go, 0)

    def gather_rest(buf, f_sem, r_sem):
        def go(q, carry):
            dev = q * CORES + (1 - core)
            send(buf.at[dev], buf.at[dev], f_sem.at[q], r_sem.at[dev], sib).wait_recv()
            return carry

        lax.fori_loop(0, chips, go, 0)

    def gather_end(buf, s_sem, f_sem, r_sem):
        def go(k, carry):
            q = peer_chip(k)
            send(buf.at[me], buf.at[me], s_sem.at[q], r_sem.at[me], sib).wait_send()
            dev = q * CORES + core
            send(buf.at[dev], buf.at[dev], f_sem.at[q], r_sem.at[me], sib).wait_send()
            return carry

        lax.fori_loop(1, chips, go, 0)
        send(buf.at[me], buf.at[me], f_sem.at[chip], r_sem.at[me], sib).wait_send()

    gather_start(gath, g_send, g_fwd, g_recv)

    own = j * CORES + core
    other = j * CORES + (1 - core)

    def c_direct(q):
        return send(centers, cbuf.at[own], c_send.at[q], c_recv.at[own], dev_of(q, z, core))

    def w_direct(q):
        return send(wts.at[q], wbuf.at[own], w_send.at[q], w_recv.at[own], dev_of(q, z, core))

    def c_pass(q):
        slot = q * CORES + core
        return send(cbuf.at[slot], cbuf.at[slot], c_fwd.at[q], c_recv.at[slot], sib)

    def w_pass(q):
        slot = q * CORES + core
        return send(wbuf.at[slot], wbuf.at[slot], w_fwd.at[q], w_recv.at[slot], sib)

    c_own = send(centers, cbuf.at[own], c_send.at[j], c_recv.at[own], sib)
    w_own = send(wts.at[j], wbuf.at[own], w_send.at[j], w_recv.at[own], sib)
    c_own.start()
    w_own.start()
    near = [lax.rem(j + k, gc) for k in range(1, gc)]
    for q in near:
        c_direct(q).start()
        w_direct(q).start()
    pair = 2 * sub_dev
    sub_col = jnp.sum(
        jnp.where(
            iota((pair, sub_dev), 0) == iota((pair, sub_dev), 1),
            sub_index[...].astype(F32), 0.0,
        ),
        axis=1, keepdims=True,
    )
    sub_hot = hot(
        (iota((pair, held), 0) < sub_dev) & (sub_col == iota((pair, held), 1).astype(F32))
    )
    eig16 = nn(
        hot(iota((pair, sub_dev), 0) == iota((pair, sub_dev), 1) + sub_dev), eigvecs[...]
    ).astype(BF16)
    eig16 = nn(eig16, hot(iota((rank, width), 0) == iota((rank, width), 1)))
    gath2[me] = (nn(sub_hot, centers[...]) + eig16).astype(BF16)

    gather_start(gath2, h_send, h_fwd, h_recv)

    bi_col = to_col(bi_row, rows_b)
    own_col = jnp.floor((bi_col + 0.5) * (1.0 / held))
    same = own_col == own_row
    rank_col = jnp.sum(jnp.where(same, jnp.where(c_i < r_i, 1.0, 0.0), 0.0), axis=1, keepdims=True)
    pos_col = own_col * share + rank_col
    order = hot(pos_col == c_i.astype(F32))
    c_sq = sq_col(centers[...])
    c_sq_row = to_row(c_sq, held)
    lab_row = labels[...].astype(F32)
    lab_buf[...] = jnp.broadcast_to(to_col(lab_row, rows_b), (rows_b, 128))
    first = core * half + z * rz
    lab_here = jnp.sum(
        jnp.where(iota((rz, rows_b), 0) + first == iota((rz, rows_b), 1), lab_row, 0.0),
        axis=1, keepdims=True,
    )

    gather_pass(gath, g_fwd, g_recv)
    gather_rest(gath, g_fwd, g_recv)

    batch[...] = nn(order, gath[...].reshape(rows_b, width)).astype(BF16)
    rows = batch[pl.ds(pl.multiple_of(core * half, half), half), :]
    rows_sq = sq_col(rows)

    def add_from(slot):
        there = cbuf[slot]
        there_sq = to_row(sq_col(there), held)
        return nt(kern(rows, there, rows_sq, there_sq), wbuf[slot])

    part[...] = nt(kern(rows, centers[...], rows_sq, c_sq_row), wts[j]).reshape(nz, rz, cs)
    send(cbuf.at[other], cbuf.at[other], c_fwd.at[j], c_recv.at[other], sib).wait_recv()
    send(wbuf.at[other], wbuf.at[other], w_fwd.at[j], w_recv.at[other], sib).wait_recv()
    part[...] += add_from(other).reshape(nz, rz, cs)
    for q in near[::-1]:
        c_pass(q).wait_recv()
        c_pass(q).start()
        w_pass(q).wait_recv()
        w_pass(q).start()
        part[...] += add_from(q * CORES + core).reshape(nz, rz, cs)
    for q in near[::-1]:
        slot = q * CORES + 1 - core
        send(cbuf.at[slot], cbuf.at[slot], c_fwd.at[q], c_recv.at[slot], sib).wait_recv()
        send(wbuf.at[slot], wbuf.at[slot], w_fwd.at[q], w_recv.at[slot], sib).wait_recv()
        part[...] += add_from(slot).reshape(nz, rz, cs)

    def sum_copy(q):
        return send(part.at[q], recv.at[z], r_send.at[q], r_recv.at[z], dev_of(j, q, core))

    along = [lax.rem(z + k, nz) for k in range(1, nz)]
    for q in along:
        sum_copy(q).start()

    b_sq_row = to_row(sq_col(batch[...]), rows_b)
    gather_pass(gath2, h_fwd, h_recv)
    kbz_t = kern(centers[...], batch[...], c_sq, b_sq_row).astype(F32)
    gather_rest(gath2, h_fwd, h_recv)
    both = gath2[...].reshape(n * pair, width)
    s_i, g_i = iota((subset, n * pair), 0), iota((subset, n * pair), 1)
    spot = s_i + lax.div(s_i, sub_dev) * sub_dev
    sub_rows = nn(hot(spot == g_i), both).astype(BF16)
    vecs = nn(hot(spot + sub_dev == g_i), both).astype(BF16)[:, :rank]
    sub_sq = sq_col(sub_rows)
    kze = nn(kern(centers[...], sub_rows, c_sq, to_row(sub_sq, subset)), vecs)
    proj = tn(vecs, kern(sub_rows, batch[...], sub_sq, b_sq_row))
    to_grad = kbz_t - nn(kze * scales[...], proj, precision=HIGHEST)
    to_sub = nn(eigvecs[...].astype(F32) * scales[...], proj, precision=HIGHEST)
    high = to_grad.astype(BF16)
    left[:held, :] = high
    left[held:2 * held, :] = (to_grad - high.astype(F32)).astype(BF16)
    sub_high = to_sub.astype(BF16).astype(F32)
    left[2 * held:, :] = jnp.concatenate([sub_high, to_sub - sub_high], axis=0).astype(BF16)

    total = part[z]
    for q in along[::-1]:
        send(part.at[q], recv.at[q], r_send.at[q], r_recv.at[q], sib).wait_recv()
        total = total + recv[q]
    lanes = iota((rz, cs), 1) + j * cs
    at_label = jnp.sum(
        jnp.where(lanes.astype(F32) == lab_here, total - 1.0, 0.0), axis=1, keepdims=True
    )
    spread = jnp.sum(
        jnp.where(iota((rz, 128), 0) == iota((rz, 128), 1), at_label, 0.0), axis=0, keepdims=True
    )
    cols = pl.ds(pl.multiple_of(j * cs, 128), cs)
    pred[core * nz + z, :, cols] = total.astype(BF16)
    fix[me] = jnp.broadcast_to(spread, (16, 128)).astype(BF16)

    def piece(t, pj, pz, pc):
        if t == 0:
            return pred.at[pc * nz + pz, :, pl.ds(pl.multiple_of(pj * cs, 128), cs)]
        return fix.at[dev_of(pj, pz, pc)]

    def pass_on(t, pj, pz, s_sem, dev):
        here = piece(t, pj, pz, core)
        return send(here, here, s_sem, p_recv.at[t, dev_of(pj, pz, core)], dev)

    def to_z(t, q):
        return pass_on(t, j, z, pz_send.at[t, q], dev_of(j, q, core))

    def to_plane(t, pz, q):
        return pass_on(t, j, pz, pp_send.at[t, pz * gc + q], dev_of(q, z, core))

    def to_sib(t, pj, pz):
        return pass_on(t, pj, pz, ps_send.at[t, pz * gc + pj], sib)

    def arrived(t, pj, pz, pc):
        here = piece(t, pj, pz, pc)
        return send(here, here, ps_send.at[t, pz * gc + pj], p_recv.at[t, dev_of(pj, pz, pc)], sib)

    for t in range(2):
        for q in along:
            to_z(t, q).start()
    for t in range(2):
        for q in near:
            to_plane(t, z, q).start()
        to_sib(t, j, z).start()
    for pz in along[::-1]:
        for t in range(2):
            arrived(t, j, pz, core).wait_recv()
            for q in near:
                to_plane(t, pz, q).start()
            to_sib(t, j, pz).start()
    def finish(pz, pc):
        lo = pl.multiple_of((pc * nz + pz) * rz, rz)
        held_pred = pred[pc * nz + pz]
        pred_out[pl.ds(lo, rz), :] = held_pred[:, :classes]
        fixes = jnp.zeros((16, 128), F32)
        for q in range(gc):
            fixes = fixes + fix[dev_of(q, pz, pc)].astype(F32)
        fix_col = jnp.sum(
            jnp.where(iota((rz, 128), 0) == iota((rz, 128), 1), fixes[:1], 0.0),
            axis=1, keepdims=True,
        )
        resid[pl.ds(lo, rz), :] = jnp.where(
            iota((rz, cp), 1).astype(F32) == lab_buf[pl.ds(lo, rz), :][:, :1],
            fix_col, held_pred.astype(F32),
        ).astype(BF16)

    def apply(pc):
        span = pl.ds(pl.multiple_of(pc * half, half), half)
        return nn(left[:, span], resid[span, :])

    for pz in [z] + along[::-1]:
        for q in near[::-1]:
            for t in range(2):
                arrived(t, q, pz, core).wait_recv()
                to_sib(t, q, pz).start()
        finish(pz, core)
    out = apply(core)
    for pz in [z] + along[::-1]:
        for q in [j] + near[::-1]:
            for t in range(2):
                arrived(t, q, pz, 1 - core).wait_recv()
        finish(pz, 1 - core)
    out = out + apply(1 - core)
    grad_out[...] = (out[:held] + out[held:2 * held]).astype(BF16)[:, :classes]
    sub_out[...] = (out[2 * held:2 * held + sub_dev] + out[2 * held + sub_dev:])[:, :classes]

    gather_end(gath, g_send, g_fwd, g_recv)
    gather_end(gath2, h_send, h_fwd, h_recv)
    c_own.wait_send()
    w_own.wait_send()
    for q in near:
        c_direct(q).wait_send()
        w_direct(q).wait_send()
        c_pass(q).wait_send()
        w_pass(q).wait_send()
    for q in along:
        sum_copy(q).wait_send()
    for t in range(2):
        for q in along:
            to_z(t, q).wait_send()
        for pz in [z] + along:
            for q in near:
                to_plane(t, pz, q).wait_send()
            for q in [j] + near:
                to_sib(t, q, pz).wait_send()


def fused(n_blk, n_grid, centers, weights, batch_index, labels, sub_index, eigvecs, scales):
    n = n_blk * n_grid
    chips = n // CORES
    held, width = centers.shape
    classes = weights.shape[1]
    rows_b = batch_index.shape[0]
    sub_dev, rank = eigvecs.shape
    share = rows_b // n
    gc, nz = n_blk * 2, n_grid // (2 * CORES)
    cs = pl.cdiv(classes, gc * 128) * 128
    rz = rows_b // (CORES * nz)
    dma = pltpu.SemaphoreType.DMA
    vmem = pl.BlockSpec(memory_space=pltpu.VMEM)
    return pl.pallas_call(
        functools.partial(body, n_blk, n_grid, share),
        out_shape=(
            jax.ShapeDtypeStruct((rows_b, classes), BF16),
            jax.ShapeDtypeStruct((held, classes), BF16),
            jax.ShapeDtypeStruct((sub_dev, classes), F32),
        ),
        in_specs=[vmem] * 7,
        out_specs=(vmem, vmem, vmem),
        scratch_shapes=[
            pltpu.VMEM((gc * CORES, held, width), BF16),
            pltpu.VMEM((gc, cs, held), BF16),
            pltpu.VMEM((gc * CORES, cs, held), BF16),
            pltpu.VMEM((n, share, width), BF16),
            pltpu.VMEM((n, 2 * sub_dev, width), BF16),
            pltpu.VMEM((rows_b, width), BF16),
            pltpu.VMEM((nz, rz, cs), F32),
            pltpu.VMEM((nz, rz, cs), F32),
            pltpu.VMEM((CORES * nz, rz, gc * cs), BF16),
            pltpu.VMEM((n, 16, 128), BF16),
            pltpu.VMEM((2 * held + 2 * sub_dev, rows_b), BF16),
            pltpu.VMEM((rows_b, gc * cs), BF16),
            pltpu.VMEM((rows_b, 128), F32),
            dma((gc,)), dma((gc,)), dma((gc * CORES,)),
            dma((gc,)), dma((gc,)), dma((gc * CORES,)),
            dma((chips,)), dma((chips,)), dma((n,)),
            dma((chips,)), dma((chips,)), dma((n,)),
            dma((2, nz)), dma((2, nz * gc)), dma((2, nz * gc)), dma((2, n)),
            dma((nz,)), dma((nz,)),
        ],
        compiler_params=pltpu.CompilerParams(
            collective_id=0, has_side_effects=True, vmem_limit_bytes=48 * 1024 * 1024
        ),
    )(
        centers, weights.T, batch_index.reshape(1, rows_b), labels.reshape(1, rows_b),
        sub_index.reshape(1, sub_dev), eigvecs, scales.reshape(1, rank),
    )


def solution(mesh):
    n_blk, n_grid = mesh.shape["blk"], mesh.shape["grid"]
    n = n_blk * n_grid

    def step(centers, *rest):
        rows_b, sub_dev = rest[1].shape[0], rest[4].shape[0]
        nz = n_grid // (2 * CORES)
        whole_tiles = (
            n_grid % (2 * CORES) == 0 and rows_b % (16 * n) == 0 and sub_dev % 8 == 0
            and rows_b <= 128 * CORES * nz and rows_b % (128 * CORES) == 0
        )
        if whole_tiles:
            return fused(n_blk, n_grid, centers, *rest)
        return local(centers, *rest)

    return jax.shard_map(
        step,
        mesh=mesh,
        in_specs=(
            P(("blk", "grid"), None),
            P(("blk", "grid"), None),
            P(),
            P(),
            P(("blk", "grid")),
            P(("blk", "grid"), None),
            P(),
        ),
        out_specs=(P(), P(("blk", "grid"), None), P(("blk", "grid"), None)),
        check_vma=False,
    )
```

```python
import functools

import jax
import jax.numpy as jnp
from jax import lax
from jax.experimental import pallas as pl
from jax.experimental.pallas import tpu as pltpu
from jax.sharding import PartitionSpec as P

SOFTEN = 1.0
SPREAD = 4.0
CORES = 2
MESH = pl.DeviceIdType.MESH
F32 = jnp.float32
BF16 = jnp.bfloat16
HIGHEST = lax.Precision.HIGHEST


def kernel(left, right):
    left_sq = jnp.sum(jnp.square(left.astype(jnp.float32)), axis=1)
    right_sq = jnp.sum(jnp.square(right.astype(jnp.float32)), axis=1)
    cross = lax.dot_general(
        left, right, (((1,), (1,)), ((), ())), preferred_element_type=jnp.float32
    )
    dist = jnp.sqrt(jnp.maximum(left_sq[:, None] + right_sq[None, :] - 2.0 * cross, 0.0) + SOFTEN)
    return jnp.exp(-dist / SPREAD)


def one_hot(label_rows, classes):
    return (label_rows[:, None] == jnp.arange(classes, dtype=jnp.int32)[None, :]).astype(
        jnp.float32
    )


def local(centers, weights, batch_index, labels, sub_index, eigvecs, scales):
    myself = lax.axis_index(("blk", "grid"))
    held = centers.shape[0]
    classes = weights.shape[1]
    owner = batch_index // held
    within = batch_index % held
    picked = jnp.take(centers, within, axis=0).astype(jnp.float32)
    picked = jnp.where((owner == myself)[:, None], picked, 0.0)
    batch = lax.psum(picked, ("blk", "grid")).astype(jnp.bfloat16)
    kbz = kernel(batch, centers).astype(jnp.bfloat16)
    partial_out = jnp.dot(kbz, weights.astype(jnp.bfloat16), preferred_element_type=jnp.float32)
    total = lax.psum(partial_out, ("blk", "grid"))
    predictions = total.astype(jnp.bfloat16)
    resid = (total - one_hot(labels, classes)).astype(jnp.bfloat16)
    subset_here = jnp.take(centers, sub_index, axis=0)
    sub_rows = lax.all_gather(subset_here, ("blk", "grid"), axis=0, tiled=True)
    vec_rows = lax.all_gather(eigvecs, ("blk", "grid"), axis=0, tiled=True)
    kzs = kernel(centers, sub_rows).astype(jnp.bfloat16)
    ksb_piece = kernel(sub_rows, batch).astype(jnp.bfloat16)
    kze_next = jnp.dot(kzs, vec_rows, preferred_element_type=jnp.float32)
    proj_next = lax.dot_general(
        vec_rows, ksb_piece, (((0,), (0,)), ((), ())), preferred_element_type=jnp.float32
    )
    coeff = jnp.dot(proj_next, resid.astype(jnp.float32), precision=lax.Precision.HIGHEST)
    scaled = scales[:, None] * coeff
    sub_increment = jnp.dot(eigvecs.astype(jnp.float32), scaled, precision=lax.Precision.HIGHEST)
    correction = jnp.dot(kze_next, scaled, precision=lax.Precision.HIGHEST)
    first = lax.dot_general(
        kbz, resid, (((0,), (0,)), ((), ())), preferred_element_type=jnp.float32
    )
    center_grad = (first - correction).astype(jnp.bfloat16)
    return (predictions, center_grad, sub_increment)


def iota(shape, dim):
    return lax.broadcasted_iota(jnp.int32, shape, dim)


def to_col(row, n):
    return jnp.sum(jnp.where(iota((n, n), 0) == iota((n, n), 1), row, 0.0), axis=1, keepdims=True)


def to_row(col, n):
    return jnp.sum(jnp.where(iota((n, n), 0) == iota((n, n), 1), col, 0.0), axis=0, keepdims=True)


def hot(mask):
    return jnp.where(mask, 1.0, 0.0).astype(BF16)


def nn(a, b, **kw):
    return jnp.dot(a, b, preferred_element_type=F32, **kw)


def nt(a, b):
    return lax.dot_general(a, b, (((1,), (1,)), ((), ())), preferred_element_type=F32)


def tn(a, b):
    return lax.dot_general(a, b, (((0,), (0,)), ((), ())), preferred_element_type=F32)


def sq_col(rows):
    return jnp.sum(jnp.square(rows.astype(F32)), axis=1, keepdims=True)


def kern(left, right, left_sq, right_sq):
    dist = jnp.sqrt(jnp.maximum(left_sq + right_sq - 2.0 * nt(left, right), 0.0) + SOFTEN)
    return jnp.exp(dist * (-1.0 / SPREAD)).astype(BF16)


def body(
    n_blk, n_grid, share,
    centers, weights_t, batch_index, labels, sub_index, eigvecs, scales,
    pred_out, grad_out, sub_out,
    cbuf, wts, wbuf, gath, gath2, batch, part, recv, pred, fix, left, resid, lab_buf,
    c_send, c_fwd, c_recv, w_send, w_fwd, w_recv, g_send, g_fwd, g_recv, h_send, h_fwd, h_recv,
    pz_send, pp_send, ps_send, p_recv, r_send, r_recv,
):
    held, width = centers.shape
    classes = weights_t.shape[0]
    rows_b = batch_index.shape[1]
    gc, cs, _ = wts.shape
    nz, rz, _ = part.shape
    cp = gc * cs
    sub_dev, rank = eigvecs.shape
    n = n_blk * n_grid
    chips = n // CORES
    subset = n * sub_dev
    half = rows_b // CORES
    blk, grid = lax.axis_index("blk"), lax.axis_index("grid")
    me = blk * n_grid + grid
    chip, core = me // CORES, lax.rem(me, CORES)
    z, j = grid // (2 * CORES), blk * 2 + lax.rem(grid // CORES, 2)

    def at(dev):
        return (dev // n_grid, lax.rem(dev, n_grid))

    def dev_of(pj, pz, pc):
        return (pj // 2) * n_grid + pz * 2 * CORES + lax.rem(pj, 2) * CORES + pc

    sib = chip * CORES + (1 - core)

    def peer_chip(k):
        return lax.rem(chip + k, chips)

    def from_chip(k):
        return lax.rem(chip + chips - k, chips)

    barrier = pltpu.get_barrier_semaphore()

    def greet(k, carry):
        pl.semaphore_signal(
            barrier, inc=1, device_id=at(peer_chip(k) * CORES + core), device_id_type=MESH
        )
        return carry

    pl.semaphore_signal(barrier, inc=1, device_id=at(sib), device_id_type=MESH)
    lax.fori_loop(1, chips, greet, 0)

    bi_row = batch_index[...].astype(F32)
    own_row = jnp.floor((bi_row + 0.5) * (1.0 / held))
    r_i, c_i = iota((rows_b, rows_b), 0), iota((rows_b, rows_b), 1)
    here_row = jnp.broadcast_to(jnp.where(own_row == me.astype(F32), 1.0, 0.0), (16, rows_b))
    ahead = nn(here_row.astype(BF16), hot(r_i < c_i))[:1]
    nth = jnp.where(own_row == me.astype(F32), ahead, -1.0)
    within = bi_row - own_row * held
    pick = hot(iota((held, rows_b), 0).astype(F32) == within)
    sel = nt(hot(iota((share, rows_b), 0).astype(F32) == nth), pick).astype(BF16)
    gath[me] = nn(sel, centers[...]).astype(BF16)

    per = cs
    for q in range(gc):
        lo, hi = q * per, min((q + 1) * per, classes)
        if hi - lo < cs:
            wts[q] = jnp.zeros((cs, held), BF16)
        if hi > lo:
            wts[q, :hi - lo, :] = weights_t[lo:hi, :].astype(BF16)

    pl.semaphore_wait(barrier, chips)

    def send(src, dst, s_sem, r_sem, dev):
        return pltpu.make_async_remote_copy(
            src_ref=src, dst_ref=dst, send_sem=s_sem, recv_sem=r_sem,
            device_id=at(dev), device_id_type=MESH,
        )

    def gather_start(buf, s_sem, f_sem, r_sem):
        def go(k, carry):
            q = peer_chip(k)
            send(buf.at[me], buf.at[me], s_sem.at[q], r_sem.at[me], q * CORES + core).start()
            return carry

        lax.fori_loop(1, chips, go, 0)
        send(buf.at[me], buf.at[me], f_sem.at[chip], r_sem.at[me], sib).start()

    def gather_pass(buf, f_sem, r_sem):
        def go(k, carry):
            q = from_chip(k)
            dev = q * CORES + core
            send(buf.at[dev], buf.at[dev], f_sem.at[q], r_sem.at[dev], sib).wait_recv()
            send(buf.at[dev], buf.at[dev], f_sem.at[q], r_sem.at[dev], sib).start()
            return carry

        lax.fori_loop(1, chips, go, 0)

    def gather_rest(buf, f_sem, r_sem):
        def go(q, carry):
            dev = q * CORES + (1 - core)
            send(buf.at[dev], buf.at[dev], f_sem.at[q], r_sem.at[dev], sib).wait_recv()
            return carry

        lax.fori_loop(0, chips, go, 0)

    def gather_end(buf, s_sem, f_sem, r_sem):
        def go(k, carry):
            q = peer_chip(k)
            send(buf.at[me], buf.at[me], s_sem.at[q], r_sem.at[me], sib).wait_send()
            dev = q * CORES + core
            send(buf.at[dev], buf.at[dev], f_sem.at[q], r_sem.at[me], sib).wait_send()
            return carry

        lax.fori_loop(1, chips, go, 0)
        send(buf.at[me], buf.at[me], f_sem.at[chip], r_sem.at[me], sib).wait_send()

    gather_start(gath, g_send, g_fwd, g_recv)

    own = j * CORES + core
    other = j * CORES + (1 - core)

    def c_direct(q):
        return send(centers, cbuf.at[own], c_send.at[q], c_recv.at[own], dev_of(q, z, core))

    def w_direct(q):
        return send(wts.at[q], wbuf.at[own], w_send.at[q], w_recv.at[own], dev_of(q, z, core))

    def c_pass(q):
        slot = q * CORES + core
        return send(cbuf.at[slot], cbuf.at[slot], c_fwd.at[q], c_recv.at[slot], sib)

    def w_pass(q):
        slot = q * CORES + core
        return send(wbuf.at[slot], wbuf.at[slot], w_fwd.at[q], w_recv.at[slot], sib)

    c_own = send(centers, cbuf.at[own], c_send.at[j], c_recv.at[own], sib)
    w_own = send(wts.at[j], wbuf.at[own], w_send.at[j], w_recv.at[own], sib)
    c_own.start()
    w_own.start()
    near = [lax.rem(j + k, gc) for k in range(1, gc)]
    for q in near:
        c_direct(q).start()
        w_direct(q).start()
    pair = 2 * sub_dev
    sub_col = jnp.sum(
        jnp.where(
            iota((pair, sub_dev), 0) == iota((pair, sub_dev), 1),
            sub_index[...].astype(F32), 0.0,
        ),
        axis=1, keepdims=True,
    )
    sub_hot = hot(
        (iota((pair, held), 0) < sub_dev) & (sub_col == iota((pair, held), 1).astype(F32))
    )
    eig16 = nn(
        hot(iota((pair, sub_dev), 0) == iota((pair, sub_dev), 1) + sub_dev), eigvecs[...]
    ).astype(BF16)
    eig16 = nn(eig16, hot(iota((rank, width), 0) == iota((rank, width), 1)))
    gath2[me] = (nn(sub_hot, centers[...]) + eig16).astype(BF16)

    gather_start(gath2, h_send, h_fwd, h_recv)

    bi_col = to_col(bi_row, rows_b)
    own_col = jnp.floor((bi_col + 0.5) * (1.0 / held))
    same = own_col == own_row
    rank_col = jnp.sum(jnp.where(same, jnp.where(c_i < r_i, 1.0, 0.0), 0.0), axis=1, keepdims=True)
    pos_col = own_col * share + rank_col
    order = hot(pos_col == c_i.astype(F32))
    c_sq = sq_col(centers[...])
    c_sq_row = to_row(c_sq, held)
    lab_row = labels[...].astype(F32)
    lab_buf[...] = jnp.broadcast_to(to_col(lab_row, rows_b), (rows_b, 128))
    first = core * half + z * rz
    lab_here = jnp.sum(
        jnp.where(iota((rz, rows_b), 0) + first == iota((rz, rows_b), 1), lab_row, 0.0),
        axis=1, keepdims=True,
    )

    gather_pass(gath, g_fwd, g_recv)
    gather_rest(gath, g_fwd, g_recv)

    batch[...] = nn(order, gath[...].reshape(rows_b, width)).astype(BF16)
    rows = batch[pl.ds(pl.multiple_of(core * half, half), half), :]
    rows_sq = sq_col(rows)

    def add_from(slot):
        there = cbuf[slot]
        there_sq = to_row(sq_col(there), held)
        return nt(kern(rows, there, rows_sq, there_sq), wbuf[slot])

    part[...] = nt(kern(rows, centers[...], rows_sq, c_sq_row), wts[j]).reshape(nz, rz, cs)
    send(cbuf.at[other], cbuf.at[other], c_fwd.at[j], c_recv.at[other], sib).wait_recv()
    send(wbuf.at[other], wbuf.at[other], w_fwd.at[j], w_recv.at[other], sib).wait_recv()
    part[...] += add_from(other).reshape(nz, rz, cs)
    for q in near[::-1]:
        c_pass(q).wait_recv()
        c_pass(q).start()
        w_pass(q).wait_recv()
        w_pass(q).start()
        part[...] += add_from(q * CORES + core).reshape(nz, rz, cs)
    for q in near[::-1]:
        slot = q * CORES + 1 - core
        send(cbuf.at[slot], cbuf.at[slot], c_fwd.at[q], c_recv.at[slot], sib).wait_recv()
        send(wbuf.at[slot], wbuf.at[slot], w_fwd.at[q], w_recv.at[slot], sib).wait_recv()
        part[...] += add_from(slot).reshape(nz, rz, cs)

    def sum_copy(q):
        return send(part.at[q], recv.at[z], r_send.at[q], r_recv.at[z], dev_of(j, q, core))

    along = [lax.rem(z + k, nz) for k in range(1, nz)]
    for q in along:
        sum_copy(q).start()

    b_sq_row = to_row(sq_col(batch[...]), rows_b)
    gather_pass(gath2, h_fwd, h_recv)
    kbz_t = kern(centers[...], batch[...], c_sq, b_sq_row).astype(F32)
    total = part[z]
    for q in along[::-1]:
        send(part.at[q], recv.at[q], r_send.at[q], r_recv.at[q], sib).wait_recv()
        total = total + recv[q]
    lanes = iota((rz, cs), 1) + j * cs
    at_label = jnp.sum(
        jnp.where(lanes.astype(F32) == lab_here, total - 1.0, 0.0), axis=1, keepdims=True
    )
    spread = jnp.sum(
        jnp.where(iota((rz, 128), 0) == iota((rz, 128), 1), at_label, 0.0), axis=0, keepdims=True
    )
    pred[me] = total.astype(BF16)
    fix[me] = jnp.broadcast_to(spread, (16, 128)).astype(BF16)

    def piece(t, pj, pz, pc):
        if t == 0:
            return pred.at[dev_of(pj, pz, pc)]
        return fix.at[dev_of(pj, pz, pc)]

    def pass_on(t, pj, pz, s_sem, dev):
        here = piece(t, pj, pz, core)
        return send(here, here, s_sem, p_recv.at[t, dev_of(pj, pz, core)], dev)

    def to_z(t, q):
        return pass_on(t, j, z, pz_send.at[t, q], dev_of(j, q, core))

    def to_plane(t, pz, q):
        return pass_on(t, j, pz, pp_send.at[t, pz * gc + q], dev_of(q, z, core))

    def to_sib(t, pj, pz):
        return pass_on(t, pj, pz, ps_send.at[t, pz * gc + pj], sib)

    def arrived(t, pj, pz, pc):
        here = piece(t, pj, pz, pc)
        return send(here, here, ps_send.at[t, pz * gc + pj], p_recv.at[t, dev_of(pj, pz, pc)], sib)

    for t in range(2):
        for q in along:
            to_z(t, q).start()
    for t in range(2):
        for q in near:
            to_plane(t, z, q).start()
        to_sib(t, j, z).start()
    for pz in along[::-1]:
        for t in range(2):
            arrived(t, j, pz, core).wait_recv()
            for q in near:
                to_plane(t, pz, q).start()
            to_sib(t, j, pz).start()
    gather_rest(gath2, h_fwd, h_recv)
    both = gath2[...].reshape(n * pair, width)
    s_i, g_i = iota((subset, n * pair), 0), iota((subset, n * pair), 1)
    spot = s_i + lax.div(s_i, sub_dev) * sub_dev
    sub_rows = nn(hot(spot == g_i), both).astype(BF16)
    vecs = nn(hot(spot + sub_dev == g_i), both).astype(BF16)[:, :rank]
    sub_sq = sq_col(sub_rows)
    kze = nn(kern(centers[...], sub_rows, c_sq, to_row(sub_sq, subset)), vecs)
    proj = tn(vecs, kern(sub_rows, batch[...], sub_sq, b_sq_row))
    to_grad = kbz_t - nn(kze * scales[...], proj, precision=HIGHEST)
    to_sub = nn(eigvecs[...].astype(F32) * scales[...], proj, precision=HIGHEST)
    high = to_grad.astype(BF16)
    left[:held, :] = high
    left[held:2 * held, :] = (to_grad - high.astype(F32)).astype(BF16)
    sub_high = to_sub.astype(BF16).astype(F32)
    left[2 * held:, :] = jnp.concatenate([sub_high, to_sub - sub_high], axis=0).astype(BF16)

    def finish(pz, pc):
        lo = pl.multiple_of((pc * nz + pz) * rz, rz)
        held_pred = jnp.concatenate([pred[dev_of(q, pz, pc)] for q in range(gc)], axis=1)
        pred_out[pl.ds(lo, rz), :] = held_pred[:, :classes]
        fixes = jnp.zeros((16, 128), F32)
        for q in range(gc):
            fixes = fixes + fix[dev_of(q, pz, pc)].astype(F32)
        fix_col = jnp.sum(
            jnp.where(iota((rz, 128), 0) == iota((rz, 128), 1), fixes[:1], 0.0),
            axis=1, keepdims=True,
        )
        resid[pl.ds(lo, rz), :] = jnp.where(
            iota((rz, cp), 1).astype(F32) == lab_buf[pl.ds(lo, rz), :][:, :1],
            fix_col, held_pred.astype(F32),
        ).astype(BF16)

    def apply(pc):
        span = pl.ds(pl.multiple_of(pc * half, half), half)
        return nn(left[:, span], resid[span, :])

    for pz in [z] + along[::-1]:
        for q in near[::-1]:
            for t in range(2):
                arrived(t, q, pz, core).wait_recv()
                to_sib(t, q, pz).start()
    for pz in [z] + along[::-1]:
        finish(pz, core)
    out = apply(core)
    for pz in [z] + along[::-1]:
        for q in [j] + near[::-1]:
            for t in range(2):
                arrived(t, q, pz, 1 - core).wait_recv()
        finish(pz, 1 - core)
    out = out + apply(1 - core)
    grad_out[...] = (out[:held] + out[held:2 * held]).astype(BF16)[:, :classes]
    sub_out[...] = (out[2 * held:2 * held + sub_dev] + out[2 * held + sub_dev:])[:, :classes]

    gather_end(gath, g_send, g_fwd, g_recv)
    gather_end(gath2, h_send, h_fwd, h_recv)
    c_own.wait_send()
    w_own.wait_send()
    for q in near:
        c_direct(q).wait_send()
        w_direct(q).wait_send()
        c_pass(q).wait_send()
        w_pass(q).wait_send()
    for q in along:
        sum_copy(q).wait_send()
    for t in range(2):
        for q in along:
            to_z(t, q).wait_send()
        for pz in [z] + along:
            for q in near:
                to_plane(t, pz, q).wait_send()
            for q in [j] + near:
                to_sib(t, q, pz).wait_send()


def fused(n_blk, n_grid, centers, weights, batch_index, labels, sub_index, eigvecs, scales):
    n = n_blk * n_grid
    chips = n // CORES
    held, width = centers.shape
    classes = weights.shape[1]
    rows_b = batch_index.shape[0]
    sub_dev, rank = eigvecs.shape
    share = rows_b // n
    gc, nz = n_blk * 2, n_grid // (2 * CORES)
    cs = pl.cdiv(classes, gc * 128) * 128
    rz = rows_b // (CORES * nz)
    dma = pltpu.SemaphoreType.DMA
    vmem = pl.BlockSpec(memory_space=pltpu.VMEM)
    return pl.pallas_call(
        functools.partial(body, n_blk, n_grid, share),
        out_shape=(
            jax.ShapeDtypeStruct((rows_b, classes), BF16),
            jax.ShapeDtypeStruct((held, classes), BF16),
            jax.ShapeDtypeStruct((sub_dev, classes), F32),
        ),
        in_specs=[vmem] * 7,
        out_specs=(vmem, vmem, vmem),
        scratch_shapes=[
            pltpu.VMEM((gc * CORES, held, width), BF16),
            pltpu.VMEM((gc, cs, held), BF16),
            pltpu.VMEM((gc * CORES, cs, held), BF16),
            pltpu.VMEM((n, share, width), BF16),
            pltpu.VMEM((n, 2 * sub_dev, width), BF16),
            pltpu.VMEM((rows_b, width), BF16),
            pltpu.VMEM((nz, rz, cs), F32),
            pltpu.VMEM((nz, rz, cs), F32),
            pltpu.VMEM((n, rz, cs), BF16),
            pltpu.VMEM((n, 16, 128), BF16),
            pltpu.VMEM((2 * held + 2 * sub_dev, rows_b), BF16),
            pltpu.VMEM((rows_b, gc * cs), BF16),
            pltpu.VMEM((rows_b, 128), F32),
            dma((gc,)), dma((gc,)), dma((gc * CORES,)),
            dma((gc,)), dma((gc,)), dma((gc * CORES,)),
            dma((chips,)), dma((chips,)), dma((n,)),
            dma((chips,)), dma((chips,)), dma((n,)),
            dma((2, nz)), dma((2, nz * gc)), dma((2, nz * gc)), dma((2, n)),
            dma((nz,)), dma((nz,)),
        ],
        compiler_params=pltpu.CompilerParams(
            collective_id=0, has_side_effects=True, vmem_limit_bytes=48 * 1024 * 1024
        ),
    )(
        centers, weights.T, batch_index.reshape(1, rows_b), labels.reshape(1, rows_b),
        sub_index.reshape(1, sub_dev), eigvecs, scales.reshape(1, rank),
    )


def solution(mesh):
    n_blk, n_grid = mesh.shape["blk"], mesh.shape["grid"]
    n = n_blk * n_grid

    def step(centers, *rest):
        rows_b, sub_dev = rest[1].shape[0], rest[4].shape[0]
        nz = n_grid // (2 * CORES)
        whole_tiles = (
            n_grid % (2 * CORES) == 0 and rows_b % (16 * n) == 0 and sub_dev % 8 == 0
            and rows_b <= 128 * CORES * nz and rows_b % (128 * CORES) == 0
        )
        if whole_tiles:
            return fused(n_blk, n_grid, centers, *rest)
        return local(centers, *rest)

    return jax.shard_map(
        step,
        mesh=mesh,
        in_specs=(
            P(("blk", "grid"), None),
            P(("blk", "grid"), None),
            P(),
            P(),
            P(("blk", "grid")),
            P(("blk", "grid"), None),
            P(),
        ),
        out_specs=(P(), P(("blk", "grid"), None), P(("blk", "grid"), None)),
        check_vma=False,
    )
```
